32 devices in a mesh: dp: 4 (over y, x), fsdp: 8 (over z, core).
Axes of the slice: x: 2, y: 2, z: 4, core: 2. Of those that a mesh axis runs over, the one named last changes fastest.
Arguments:
- tokens: bfloat16 [4096, 768], P(('dp', 'fsdp')), may hold values from -6 to 6
- cotangent: bfloat16 [4096, 768], P(('dp', 'fsdp')), may hold values from -6 to 6
- segments: int32 [32, 128], P(('dp', 'fsdp')), may hold values from 0 to 7, never falling along the last dimension, each value on 1 to 64 neighbouring positions
- w_qkv: float32 [768, 2304], P(('dp', 'fsdp')), may hold values from -0.21875 to 0.21875
- w_out: float32 [768, 768], P(('dp', 'fsdp')), may hold values from -0.4375 to 0.4375
- w_up: float32 [768, 3072], P(('dp', 'fsdp')), may hold values from -0.21875 to 0.21875
- w_down: float32 [3072, 768], P(('dp', 'fsdp')), may hold values from -0.109375 to 0.109375
- vectors: float32 [9984], P(('dp', 'fsdp')), may hold values from -0.9 to 1.5
- first_qkv: float32 [768, 2304], P(('dp', 'fsdp')), may hold values from -1 to 1
- first_out: float32 [768, 768], P(('dp', 'fsdp')), may hold values from -1 to 1
- first_up: float32 [768, 3072], P(('dp', 'fsdp')), may hold values from -1 to 1
- first_down: float32 [3072, 768], P(('dp', 'fsdp')), may hold values from -1 to 1
- first_vec: float32 [9984], P(('dp', 'fsdp')), may hold values from -1 to 1
- second_qkv: float32 [768, 2304], P(('dp', 'fsdp')), may hold values from 0.02 to 0.2
- second_out: float32 [768, 768], P(('dp', 'fsdp')), may hold values from 0.02 to 0.2
- second_up: float32 [768, 3072], P(('dp', 'fsdp')), may hold values from 0.02 to 0.2
- second_down: float32 [3072, 768], P(('dp', 'fsdp')), may hold values from 0.02 to 0.2
- second_vec: float32 [9984], P(('dp', 'fsdp')), may hold values from 0.02 to 0.2
Outputs:
- output: bfloat16 [4096, 768], P(('dp', 'fsdp'))
- grad_tokens: bfloat16 [4096, 768], P(('dp', 'fsdp'))
- grad_w_qkv: float32 [768, 2304], P(('dp', 'fsdp'))
- grad_w_out: float32 [768, 768], P(('dp', 'fsdp'))
- grad_w_up: float32 [768, 3072], P(('dp', 'fsdp'))
- grad_w_down: float32 [3072, 768], P(('dp', 'fsdp'))
- grad_vectors: float32 [9984], P(('dp', 'fsdp'))
- new_w_qkv: float32 [768, 2304], P(('dp', 'fsdp'))
- new_w_out: float32 [768, 768], P(('dp', 'fsdp'))
- new_w_up: float32 [768, 3072], P(('dp', 'fsdp'))
- new_w_down: float32 [3072, 768], P(('dp', 'fsdp'))
- new_vectors: float32 [9984], P(('dp', 'fsdp'))
- new_first_qkv: float32 [768, 2304], P(('dp', 'fsdp'))
- new_first_out: float32 [768, 768], P(('dp', 'fsdp'))
- new_first_up: float32 [768, 3072], P(('dp', 'fsdp'))
- new_first_down: float32 [3072, 768], P(('dp', 'fsdp'))
- new_first_vec: float32 [9984], P(('dp', 'fsdp'))
- new_second_qkv: float32 [768, 2304], P(('dp', 'fsdp'))
- new_second_out: float32 [768, 768], P(('dp', 'fsdp'))
- new_second_up: float32 [768, 3072], P(('dp', 'fsdp'))
- new_second_down: float32 [3072, 768], P(('dp', 'fsdp'))
- new_second_vec: float32 [9984], P(('dp', 'fsdp'))
The draws below stay inside these ranges and needn't reach their ends.
Inputs may be any that keep to these rules, and one draw needn't show every extreme that they name: `segments`: in each row the numbers never fall; every number 0 to 7 names 1 to 64 consecutive tokens, and one names exactly 64.
All inputs are finite; a program needn't handle non-finite values.
Results may differ from the reference program's by a relative error of at most 0.012.
Values may be sent and summed in bfloat16 or wider, within the bound.
A program may use at most 128 MiB of HBM per device.

```python
import math
import jax
import jax.numpy as jnp
import numpy as np
from jax import lax

D = 768
HEADS = 12
HEAD_DIM = 64
ROT = 16
FF = 3072
ROWS = 128
SEGS = 8
STEP = 3
MOST = 64
TOKENS = 4096
DEVICES = 32


def draw_vectors(key, part):
    key_gain, key_shift = jax.random.split(key)
    row_index = jnp.arange(13 * D, dtype=jnp.int32) // D
    is_gain = (row_index == 0) | (row_index == 2)
    gain_draw = 1.0 + 0.5 * jnp.clip(jax.random.normal(key_gain, (13 * D,), jnp.float32), -1.0, 1.0)
    shift_draw = 0.3 * jnp.clip(jax.random.normal(key_shift, (13 * D,), jnp.float32), -3.0, 3.0)
    return jnp.where(is_gain, gain_draw, shift_draw)


def shard_levels(key, dims, shards, least, high):
    factor_of, own = 1.0, jax.random.fold_in(key, 6)
    for dim, parts in shards:
        steps = jnp.exp(jax.random.uniform(jax.random.fold_in(own, dim), (parts,), jnp.float32, least / len(shards), high / len(shards)))
        factor_of = factor_of * jnp.repeat(steps, dims[dim] // parts).reshape([-1 if axis == dim else 1 for axis in range(len(dims))])
    return factor_of


def profile(number_of, total, limit, skew):
    weights = [(1 << 20) // math.isqrt(standing ** skew) + 1 for standing in range(2, number_of + 1)]
    surplus, given = total - limit - (number_of - 1), [1] * (number_of - 1)
    while surplus > 0:
        free = [i for i in range(number_of - 1) if given[i] < limit]
        pool, budget = sum([weights[i] for i in free]), surplus
        for i in free:
            extra = min(limit - given[i], max(1, budget * weights[i] // pool), surplus)
            given[i] = given[i] + extra
            surplus = surplus - extra
    return np.array([limit] + given)


def ragged(own_key, number_of, total, limit, lean):
    if number_of == 2:
        one = jax.random.randint(own_key, (), max(1, total - limit), min(limit, total - 1) + 1)
        return jnp.stack([one, total - one])
    lengths = jnp.asarray(profile(number_of, total, limit, lean), jnp.int32)
    pairs = (number_of - 1) // 2
    donor, receiver = lengths[1:1 + 2 * pairs:2], lengths[2:2 + 2 * pairs:2]
    room = jnp.minimum(donor - 1, limit - receiver)
    moved = jax.random.randint(jax.random.fold_in(own_key, 1), (pairs,), 0, 1 << 20) % (room + 1)
    lengths = lengths.at[1:1 + 2 * pairs:2].set(donor - moved).at[2:2 + 2 * pairs:2].set(receiver + moved)
    return lengths[jax.random.permutation(jax.random.fold_in(own_key, 2), number_of)]


def normal_values(own_key, extent, width, limit, cuts=(), held_as=jnp.bfloat16):
    factor_of = shard_levels(own_key, extent, cuts, -0.22, 0.18) if cuts else 1.0
    array = jax.random.normal(own_key, extent, jnp.float32) * width * factor_of
    return jnp.minimum(jnp.maximum(array, -limit), limit).astype(held_as)


def setup_inputs(seed: int = 0) -> dict:
    seeds = jax.random.split(jax.random.key(seed), 19)
    return {
        "tokens": normal_values(seeds[0], (TOKENS, D), 1.0, 6.0, ((0, 32),)),
        "cotangent": normal_values(seeds[1], (TOKENS, D), 1.0, 6.0, ((0, 32),)),
        "segments": jax.vmap(lambda own: jnp.searchsorted(jnp.cumsum(ragged(own, SEGS, ROWS, MOST, 2)), jnp.arange(ROWS), side="right"))(jax.random.split(seeds[2], DEVICES)).reshape((DEVICES, ROWS)).astype(jnp.int32),
        "w_qkv": normal_values(seeds[3], (D, 3 * D), D ** -0.5, 0.21875, ((0, 32),), jnp.float32),
        "w_out": normal_values(seeds[4], (D, D), (D // 4) ** -0.5, 0.4375, ((0, 32),), jnp.float32),
        "w_up": normal_values(seeds[5], (D, FF), D ** -0.5, 0.21875, ((0, 32),), jnp.float32),
        "w_down": normal_values(seeds[6], (FF, D), FF ** -0.5, 0.109375, ((0, 32),), jnp.float32),
        "vectors": draw_vectors(jax.random.fold_in(seeds[18], 71), 0),
        "first_qkv": normal_values(seeds[8], (D, 3 * D), 0.2, 1.0, ((0, 32),), jnp.float32),
        "first_out": normal_values(seeds[9], (D, D), 0.2, 1.0, ((0, 32),), jnp.float32),
        "first_up": normal_values(seeds[10], (D, FF), 0.2, 1.0, ((0, 32),), jnp.float32),
        "first_down": normal_values(seeds[11], (FF, D), 0.2, 1.0, ((0, 32),), jnp.float32),
        "first_vec": normal_values(seeds[12], (13 * D,), 0.2, 1.0, ((0, 32),), jnp.float32),
        "second_qkv": jnp.clip(jnp.exp(math.log(0.2) - 2.3025851 * jax.random.uniform(seeds[13], (D, 3 * D), jnp.float32) ** shard_levels(seeds[13], (D, 3 * D), ((0, 32),), -0.2, 0.2)), 0.02, 0.2),
        "second_out": jnp.clip(jnp.exp(math.log(0.2) - 2.3025851 * jax.random.uniform(seeds[14], (D, D), jnp.float32) ** shard_levels(seeds[14], (D, D), ((0, 32),), -0.2, 0.2)), 0.02, 0.2),
        "second_up": jnp.clip(jnp.exp(math.log(0.2) - 2.3025851 * jax.random.uniform(seeds[15], (D, FF), jnp.float32) ** shard_levels(seeds[15], (D, FF), ((0, 32),), -0.2, 0.2)), 0.02, 0.2),
        "second_down": jnp.clip(jnp.exp(math.log(0.2) - 2.3025851 * jax.random.uniform(seeds[16], (FF, D), jnp.float32) ** shard_levels(seeds[16], (FF, D), ((0, 32),), -0.2, 0.2)), 0.02, 0.2),
        "second_vec": jnp.clip(jnp.exp(math.log(0.2) - 2.3025851 * jax.random.uniform(seeds[17], (13 * D,), jnp.float32) ** shard_levels(seeds[17], (13 * D,), ((0, 32),), -0.2, 0.2)), 0.02, 0.2),
    }


eps_norm = 1e-05
beta_first = 0.9
beta_second = 0.95
adam_epsilon = 1e-08
rate_matrix = 0.008
rate_vector = 0.1
decay_matrix = 0.01
rotary_base = 10000.0
mask_fill = -1e+30

def layer_norm(inputs, gain_row, offset):
    center = inputs - lax.optimization_barrier(jnp.mean(inputs, axis=-1, keepdims=True))
    inv_sigma = lax.rsqrt(lax.optimization_barrier(jnp.mean(center * center, axis=-1, keepdims=True)) + eps_norm)
    normed = center * inv_sigma
    return (normed, inv_sigma, normed * gain_row + offset)

def layer_norm_back(grad_norm, normed, inv_sigma, gain_row):
    scaled = grad_norm * gain_row
    return inv_sigma * (scaled - lax.optimization_barrier(jnp.mean(scaled, axis=-1, keepdims=True)) - normed * lax.optimization_barrier(jnp.mean(scaled * normed, axis=-1, keepdims=True)))

def gelu_value(inputs):
    return 0.5 * inputs * (1.0 + jax.scipy.special.erf(inputs * (1.0 / math.sqrt(2.0))))

def gelu_slope(inputs):
    cumulative = 0.5 * (1.0 + jax.scipy.special.erf(inputs * (1.0 / math.sqrt(2.0))))
    return cumulative + inputs * jnp.exp(-0.5 * inputs * inputs) * (1.0 / math.sqrt(2.0 * math.pi))

def rotary_tables(segment):
    rows_here = segment.shape[0]
    earlier = lax.optimization_barrier(jnp.sum((segment[None, :] < segment[:, None]).astype(jnp.int32), axis=1)).astype(jnp.int32)
    position = jnp.arange(rows_here, dtype=jnp.int32) - earlier
    half_rot = ROT // 2
    inverse = rotary_base ** (-2.0 * jnp.arange(half_rot, dtype=jnp.float32) / ROT)
    angles = position.astype(jnp.float32)[:, None] * inverse[None, :]
    return (jnp.cos(angles)[:, None, :], jnp.sin(angles)[:, None, :])

def rotate(tensor, cosine_part, sine_part):
    half_rot = ROT // 2
    front_part = tensor[..., :half_rot]
    middle = tensor[..., half_rot:ROT]
    remain = tensor[..., ROT:]
    return jnp.concatenate([front_part * cosine_part - middle * sine_part, middle * cosine_part + front_part * sine_part, remain], axis=-1)

def rotate_back(tensor, cosine_part, sine_part):
    half_rot = ROT // 2
    front_part = tensor[..., :half_rot]
    middle = tensor[..., half_rot:ROT]
    remain = tensor[..., ROT:]
    return jnp.concatenate([front_part * cosine_part + middle * sine_part, middle * cosine_part - front_part * sine_part, remain], axis=-1)

def doc_mask(segment):
    row_index = jnp.arange(segment.shape[0], dtype=jnp.int32)
    return (segment[:, None] == segment[None, :]) & (row_index[None, :] <= row_index[:, None])

def masked_scores(queries, key_rot, allowed):
    scores = jnp.einsum('qhd,khd->hqk', queries.astype(jnp.float32), key_rot.astype(jnp.float32)) * (1.0 / math.sqrt(HEAD_DIM))
    return jnp.where(allowed[None, :, :], scores, mask_fill)

def block_pass(tokens, cotangent, segment, low_qkv, low_out, low_up, low_down, low_vec):
    rows_here = tokens.shape[0]
    vec_table = low_vec.astype(jnp.float32).reshape(13, D)
    inputs = tokens.astype(jnp.float32)
    normed_one, sigma_one, hidden_one = layer_norm(inputs, vec_table[0], vec_table[1])
    normed_two, sigma_two, hidden_two = layer_norm(inputs, vec_table[2], vec_table[3])
    hidden_one = hidden_one.astype(jnp.bfloat16)
    hidden_two = hidden_two.astype(jnp.bfloat16)
    projected = jnp.dot(hidden_one, low_qkv, preferred_element_type=jnp.float32) + vec_table[4:7].reshape(-1)
    cosine_part, sine_part = rotary_tables(segment)
    queries = rotate(projected[:, :D].reshape(rows_here, HEADS, HEAD_DIM), cosine_part, sine_part).astype(jnp.bfloat16)
    key_rot = rotate(projected[:, D:2 * D].reshape(rows_here, HEADS, HEAD_DIM), cosine_part, sine_part).astype(jnp.bfloat16)
    values = projected[:, 2 * D:].reshape(rows_here, HEADS, HEAD_DIM).astype(jnp.bfloat16)
    allowed = doc_mask(segment)
    scores = masked_scores(queries, key_rot, allowed)
    top_score = lax.optimization_barrier(jnp.max(scores, axis=-1, keepdims=True))
    log_total = top_score + jnp.log(lax.optimization_barrier(jnp.sum(jnp.exp(scores - top_score), axis=-1, keepdims=True)))
    soft_weights = jnp.exp(scores - log_total).astype(jnp.bfloat16)
    context = jnp.einsum('hqk,khd->qhd', soft_weights.astype(jnp.float32), values.astype(jnp.float32)).reshape(rows_here, D).astype(jnp.bfloat16)
    attended = jnp.dot(context, low_out, preferred_element_type=jnp.float32) + vec_table[7]
    up_proj = jnp.dot(hidden_two, low_up, preferred_element_type=jnp.float32) + vec_table[8:12].reshape(-1)
    activated = gelu_value(up_proj).astype(jnp.bfloat16)
    feed_out = jnp.dot(activated, low_down, preferred_element_type=jnp.float32) + vec_table[12]
    output = (inputs + attended + feed_out).astype(jnp.bfloat16)
    grad_out = cotangent.astype(jnp.float32)
    grad_w_down = jnp.dot(activated.T, cotangent, preferred_element_type=jnp.float32)
    grad_act = jnp.dot(cotangent, low_down.T, preferred_element_type=jnp.float32)
    grad_up = grad_act * gelu_slope(up_proj)
    grad_up_low = grad_up.astype(jnp.bfloat16)
    grad_w_up = jnp.dot(hidden_two.T, grad_up_low, preferred_element_type=jnp.float32)
    grad_hidden_two = jnp.dot(grad_up_low, low_up.T, preferred_element_type=jnp.float32)
    grad_w_out = jnp.dot(context.T, cotangent, preferred_element_type=jnp.float32)
    grad_context = jnp.dot(cotangent, low_out.T, preferred_element_type=jnp.float32).astype(jnp.bfloat16).reshape(rows_here, HEADS, HEAD_DIM)
    again_scores = masked_scores(queries, key_rot, allowed)
    probs_full = jnp.exp(again_scores - log_total)
    grad_probs = jnp.einsum('qhd,khd->hqk', grad_context.astype(jnp.float32), values.astype(jnp.float32))
    row_inner = lax.optimization_barrier(jnp.sum(probs_full * grad_probs, axis=-1, keepdims=True))
    grad_scores = (probs_full * (grad_probs - row_inner) * (1.0 / math.sqrt(HEAD_DIM))).astype(jnp.bfloat16)
    grad_queries = jnp.einsum('hqk,khd->qhd', grad_scores.astype(jnp.float32), key_rot.astype(jnp.float32))
    grad_keys = jnp.einsum('hqk,qhd->khd', grad_scores.astype(jnp.float32), queries.astype(jnp.float32))
    grad_values = jnp.einsum('hqk,qhd->khd', soft_weights.astype(jnp.float32), grad_context.astype(jnp.float32))
    grad_projected = jnp.concatenate([rotate_back(grad_queries, cosine_part, sine_part).reshape(rows_here, D), rotate_back(grad_keys, cosine_part, sine_part).reshape(rows_here, D), grad_values.reshape(rows_here, D)], axis=1)
    grad_proj_low = grad_projected.astype(jnp.bfloat16)
    grad_w_qkv = jnp.dot(hidden_one.T, grad_proj_low, preferred_element_type=jnp.float32)
    grad_hidden_one = jnp.dot(grad_proj_low, low_qkv.T, preferred_element_type=jnp.float32)
    grad_table = jnp.concatenate([lax.optimization_barrier(jnp.sum(grad_hidden_one * normed_one, axis=0))[None], lax.optimization_barrier(jnp.sum(grad_hidden_one, axis=0))[None], lax.optimization_barrier(jnp.sum(grad_hidden_two * normed_two, axis=0))[None], lax.optimization_barrier(jnp.sum(grad_hidden_two, axis=0))[None], lax.optimization_barrier(jnp.sum(grad_projected, axis=0)).reshape(3, D), lax.optimization_barrier(jnp.sum(grad_out, axis=0))[None], lax.optimization_barrier(jnp.sum(grad_up, axis=0)).reshape(4, D), lax.optimization_barrier(jnp.sum(grad_out, axis=0))[None]], axis=0)
    grad_tokens = (grad_out + layer_norm_back(grad_hidden_one, normed_one, sigma_one, vec_table[0]) + layer_norm_back(grad_hidden_two, normed_two, sigma_two, vec_table[2])).astype(jnp.bfloat16)
    return (output, grad_tokens, (grad_w_qkv, grad_w_out, grad_w_up, grad_w_down, grad_table.reshape(-1)))

def adam_update(weight, gradient, moment_one, moment_two, rate_value, decay_value):
    new_one = beta_first * moment_one + (1.0 - beta_first) * gradient
    new_two = beta_second * moment_two + (1.0 - beta_second) * gradient * gradient
    corrected_one = new_one / (1.0 - beta_first ** STEP)
    corrected_two = new_two / (1.0 - beta_second ** STEP)
    new_weight = weight - rate_value * (corrected_one / (jnp.sqrt(corrected_two) + adam_epsilon) + decay_value * weight)
    return (new_weight, new_one, new_two)

def reference(tokens, cotangent, segments, w_qkv, w_out, w_up, w_down, vectors, first_qkv, first_out, first_up, first_down, first_vec, second_qkv, second_out, second_up, second_down, second_vec):
    device_count = segments.shape[0]
    group_size = max(1, min(device_count, 4096 // ROWS))
    low_qkv = w_qkv.astype(jnp.bfloat16)
    low_out = w_out.astype(jnp.bfloat16)
    low_up = w_up.astype(jnp.bfloat16)
    low_down = w_down.astype(jnp.bfloat16)
    low_vec = vectors.astype(jnp.bfloat16)
    token_blocks = tokens.reshape(device_count // group_size, group_size, ROWS, D)
    cot_blocks = cotangent.reshape(device_count // group_size, group_size, ROWS, D)
    seg_blocks = segments.reshape(device_count // group_size, group_size, ROWS)
    batched = jax.vmap(block_pass, in_axes=(0, 0, 0, None, None, None, None, None))

    def scan_step(running, block_data):
        outputs, grad_rows, grads = batched(block_data[0], block_data[1], block_data[2], low_qkv, low_out, low_up, low_down, low_vec)
        running = tuple((summed + member.sum(axis=0) for summed, member in zip(running, grads)))
        return (running, (outputs, grad_rows))
    initial = tuple((jnp.zeros(matrix.shape, jnp.float32) for matrix in (w_qkv, w_out, w_up, w_down, vectors)))
    totals, (outputs, grad_rows) = lax.scan(scan_step, initial, (token_blocks, cot_blocks, seg_blocks))
    factor = float(TOKENS) ** (-0.5)
    grad_w_qkv = totals[0] * factor
    grad_w_out = totals[1] * factor
    grad_w_up = totals[2] * factor
    grad_w_down = totals[3] * factor
    grad_vectors = totals[4] * factor
    new_w_qkv, new_first_qkv, new_second_qkv = adam_update(w_qkv, grad_w_qkv, first_qkv, second_qkv, rate_matrix, decay_matrix)
    new_w_out, new_first_out, new_second_out = adam_update(w_out, grad_w_out, first_out, second_out, rate_matrix, decay_matrix)
    new_w_up, new_first_up, new_second_up = adam_update(w_up, grad_w_up, first_up, second_up, rate_matrix, decay_matrix)
    new_w_down, new_first_down, new_second_down = adam_update(w_down, grad_w_down, first_down, second_down, rate_matrix, decay_matrix)
    new_vectors, new_first_vec, new_second_vec = adam_update(vectors, grad_vectors, first_vec, second_vec, rate_vector, 0.0)
    output = outputs.reshape(TOKENS, D)
    grad_tokens = grad_rows.reshape(TOKENS, D)
    return (output, grad_tokens, grad_w_qkv, grad_w_out, grad_w_up, grad_w_down, grad_vectors, new_w_qkv, new_w_out, new_w_up, new_w_down, new_vectors, new_first_qkv, new_first_out, new_first_up, new_first_down, new_first_vec, new_second_qkv, new_second_out, new_second_up, new_second_down, new_second_vec)
```

```python
import functools
import math

import jax
import jax.numpy as jnp
from jax import lax
from jax.experimental import pallas as pl
from jax.experimental.pallas import tpu as pltpu
from jax.sharding import PartitionSpec as P

D = 768
HEADS = 12
HEAD_DIM = 64
ROT = 16
STEP = 3


eps_norm = 1e-05
beta_first = 0.9
beta_second = 0.95
adam_epsilon = 1e-08
rate_matrix = 0.008
rate_vector = 0.1
decay_matrix = 0.01
rotary_base = 10000.0
mask_fill = -1e30


def layer_norm(inputs, gain_row, offset):
    center = inputs - jnp.mean(inputs, axis=-1, keepdims=True)
    inv_sigma = lax.rsqrt(jnp.mean(center * center, axis=-1, keepdims=True) + eps_norm)
    normed = center * inv_sigma
    return (normed, inv_sigma, normed * gain_row + offset)


def layer_norm_back(grad_norm, normed, inv_sigma, gain_row):
    scaled = grad_norm * gain_row
    return inv_sigma * (
        scaled
        - jnp.mean(scaled, axis=-1, keepdims=True)
        - normed * jnp.mean(scaled * normed, axis=-1, keepdims=True)
    )


def gelu_value(inputs):
    return 0.5 * inputs * (1.0 + jax.scipy.special.erf(inputs * (1.0 / math.sqrt(2.0))))


def gelu_slope(inputs):
    cumulative = 0.5 * (1.0 + jax.scipy.special.erf(inputs * (1.0 / math.sqrt(2.0))))
    return cumulative + inputs * jnp.exp(-0.5 * inputs * inputs) * (1.0 / math.sqrt(2.0 * math.pi))


def rotary_tables(segment):
    rows_here = segment.shape[0]
    earlier = jnp.sum((segment[None, :] < segment[:, None]).astype(jnp.int32), axis=1)
    position = jnp.arange(rows_here, dtype=jnp.int32) - earlier
    half_rot = ROT // 2
    inverse = rotary_base ** (-2.0 * jnp.arange(half_rot, dtype=jnp.float32) / ROT)
    angles = position.astype(jnp.float32)[:, None] * inverse[None, :]
    return (jnp.cos(angles)[:, None, :], jnp.sin(angles)[:, None, :])


def rotate(tensor, cosine_part, sine_part):
    half_rot = ROT // 2
    front_part = tensor[..., :half_rot]
    middle = tensor[..., half_rot:ROT]
    remain = tensor[..., ROT:]
    return jnp.concatenate(
        [
            front_part * cosine_part - middle * sine_part,
            middle * cosine_part + front_part * sine_part,
            remain,
        ],
        axis=-1,
    )


def rotate_back(tensor, cosine_part, sine_part):
    half_rot = ROT // 2
    front_part = tensor[..., :half_rot]
    middle = tensor[..., half_rot:ROT]
    remain = tensor[..., ROT:]
    return jnp.concatenate(
        [
            front_part * cosine_part + middle * sine_part,
            middle * cosine_part - front_part * sine_part,
            remain,
        ],
        axis=-1,
    )


def doc_mask(segment):
    row_index = jnp.arange(segment.shape[0], dtype=jnp.int32)
    return (segment[:, None] == segment[None, :]) & (row_index[None, :] <= row_index[:, None])


def masked_scores(queries, key_rot, allowed):
    scores = jnp.einsum("qhd,khd->hqk", queries, key_rot, preferred_element_type=jnp.float32) * (
        1.0 / math.sqrt(HEAD_DIM)
    )
    return jnp.where(allowed[None, :, :], scores, mask_fill)


def forward_pass(
    tokens, allowed, cosine_part, sine_part, full_qkv, full_out, full_up, full_down, full_vec
):
    rows_here = tokens.shape[0]
    vec_table = full_vec.astype(jnp.float32).reshape(13, D)
    inputs = tokens.astype(jnp.float32)
    normed_one, sigma_one, hidden_one = layer_norm(inputs, vec_table[0], vec_table[1])
    normed_two, sigma_two, hidden_two = layer_norm(inputs, vec_table[2], vec_table[3])
    hidden_one = hidden_one.astype(jnp.bfloat16)
    hidden_two = hidden_two.astype(jnp.bfloat16)
    projected = jnp.dot(hidden_one, full_qkv, preferred_element_type=jnp.float32) + vec_table[
        4:7
    ].reshape(-1)
    queries = rotate(
        projected[:, :D].reshape(rows_here, HEADS, HEAD_DIM), cosine_part, sine_part
    ).astype(jnp.bfloat16)
    key_rot = rotate(
        projected[:, D : 2 * D].reshape(rows_here, HEADS, HEAD_DIM), cosine_part, sine_part
    ).astype(jnp.bfloat16)
    values = projected[:, 2 * D :].reshape(rows_here, HEADS, HEAD_DIM).astype(jnp.bfloat16)
    scores = masked_scores(queries, key_rot, allowed)
    top_score = jnp.max(scores, axis=-1, keepdims=True)
    log_total = top_score + jnp.log(jnp.sum(jnp.exp(scores - top_score), axis=-1, keepdims=True))
    soft_weights = jnp.exp(scores - log_total).astype(jnp.bfloat16)
    context = (
        jnp.einsum("hqk,khd->qhd", soft_weights, values, preferred_element_type=jnp.float32)
        .reshape(rows_here, D)
        .astype(jnp.bfloat16)
    )
    attended = jnp.dot(context, full_out, preferred_element_type=jnp.float32) + vec_table[7]
    up_proj = jnp.dot(hidden_two, full_up, preferred_element_type=jnp.float32) + vec_table[
        8:12
    ].reshape(-1)
    activated = gelu_value(up_proj).astype(jnp.bfloat16)
    feed_out = jnp.dot(activated, full_down, preferred_element_type=jnp.float32) + vec_table[12]
    output = (inputs + attended + feed_out).astype(jnp.bfloat16)
    saved = (
        normed_one,
        sigma_one,
        hidden_one,
        normed_two,
        sigma_two,
        hidden_two,
        queries,
        key_rot,
        values,
        log_total,
        context,
        up_proj,
        activated,
    )
    return (output, saved)


def backward_pass(
    saved,
    cotangent,
    allowed,
    cosine_part,
    sine_part,
    back_qkv,
    back_out,
    back_up,
    back_down,
    back_vec,
):
    (
        normed_one,
        sigma_one,
        hidden_one,
        normed_two,
        sigma_two,
        hidden_two,
        queries,
        key_rot,
        values,
        log_total,
        context,
        up_proj,
        activated,
    ) = saved
    rows_here = cotangent.shape[0]
    vec_table = back_vec.astype(jnp.float32).reshape(13, D)
    grad_out = cotangent.astype(jnp.float32)
    grad_w_down = jnp.dot(activated.T, cotangent, preferred_element_type=jnp.float32)
    grad_act = jnp.dot(cotangent, back_down.T, preferred_element_type=jnp.float32)
    grad_up = grad_act * gelu_slope(up_proj)
    grad_up_low = grad_up.astype(jnp.bfloat16)
    grad_w_up = jnp.dot(hidden_two.T, grad_up_low, preferred_element_type=jnp.float32)
    grad_hidden_two = jnp.dot(grad_up_low, back_up.T, preferred_element_type=jnp.float32)
    grad_w_out = jnp.dot(context.T, cotangent, preferred_element_type=jnp.float32)
    grad_context = (
        jnp.dot(cotangent, back_out.T, preferred_element_type=jnp.float32)
        .astype(jnp.bfloat16)
        .reshape(rows_here, HEADS, HEAD_DIM)
    )
    again_scores = masked_scores(queries, key_rot, allowed)
    probs_full = jnp.exp(again_scores - log_total)
    probs_low = probs_full.astype(jnp.bfloat16)
    grad_probs = jnp.einsum(
        "qhd,khd->hqk", grad_context, values, preferred_element_type=jnp.float32
    )
    row_inner = jnp.sum(probs_full * grad_probs, axis=-1, keepdims=True)
    grad_scores = (probs_full * (grad_probs - row_inner) * (1.0 / math.sqrt(HEAD_DIM))).astype(
        jnp.bfloat16
    )
    grad_queries = jnp.einsum(
        "hqk,khd->qhd", grad_scores, key_rot, preferred_element_type=jnp.float32
    )
    grad_keys = jnp.einsum("hqk,qhd->khd", grad_scores, queries, preferred_element_type=jnp.float32)
    grad_values = jnp.einsum(
        "hqk,qhd->khd", probs_low, grad_context, preferred_element_type=jnp.float32
    )
    grad_projected = jnp.concatenate(
        [
            rotate_back(grad_queries, cosine_part, sine_part).reshape(rows_here, D),
            rotate_back(grad_keys, cosine_part, sine_part).reshape(rows_here, D),
            grad_values.reshape(rows_here, D),
        ],
        axis=1,
    )
    grad_proj_low = grad_projected.astype(jnp.bfloat16)
    grad_w_qkv = jnp.dot(hidden_one.T, grad_proj_low, preferred_element_type=jnp.float32)
    grad_hidden_one = jnp.dot(grad_proj_low, back_qkv.T, preferred_element_type=jnp.float32)
    grad_table = jnp.concatenate(
        [
            jnp.sum(grad_hidden_one * normed_one, axis=0)[None],
            jnp.sum(grad_hidden_one, axis=0)[None],
            jnp.sum(grad_hidden_two * normed_two, axis=0)[None],
            jnp.sum(grad_hidden_two, axis=0)[None],
            jnp.sum(grad_projected, axis=0).reshape(3, D),
            jnp.sum(grad_out, axis=0)[None],
            jnp.sum(grad_up, axis=0).reshape(4, D),
            jnp.sum(grad_out, axis=0)[None],
        ],
        axis=0,
    )
    grad_tokens = (
        grad_out
        + layer_norm_back(grad_hidden_one, normed_one, sigma_one, vec_table[0])
        + layer_norm_back(grad_hidden_two, normed_two, sigma_two, vec_table[2])
    ).astype(jnp.bfloat16)
    return (grad_tokens, grad_w_qkv, grad_w_out, grad_w_up, grad_w_down, grad_table.reshape(-1))


def adam_update(weight, gradient, moment_one, moment_two, rate_value, decay_value):
    new_one = beta_first * moment_one + (1.0 - beta_first) * gradient
    new_two = beta_second * moment_two + (1.0 - beta_second) * gradient * gradient
    corrected_one = new_one / (1.0 - beta_first**STEP)
    corrected_two = new_two / (1.0 - beta_second**STEP)
    new_weight = weight - rate_value * (
        corrected_one / (jnp.sqrt(corrected_two) + adam_epsilon) + decay_value * weight
    )
    return (new_weight, new_one, new_two)


MESH = pl.DeviceIdType.MESH
LANES = 128
VEC_WIDE = 3 * LANES
STEP_WIDE = 5 * LANES


class Place:
    def __init__(self, side, fsdp):
        self.side, self.fsdp, self.depth = side, fsdp, fsdp // 2
        index, column = lax.axis_index("dp"), lax.axis_index("fsdp")
        self.core, self.level = lax.rem(column, 2), lax.div(column, 2)
        self.high, self.low = lax.div(index, side), lax.rem(index, side)

    def device(self, first, second, level, owner=None, target=None):
        owner = self.core if owner is None else owner
        target = owner if target is None else target
        one = lax.rem(self.low * (1 - owner) + self.high * owner + first, self.side)
        two = lax.rem(self.high * (1 - owner) + self.low * owner + second, self.side)
        high = two * (1 - owner) + one * owner
        low = one * (1 - owner) + two * owner
        return (high * self.side + low, lax.rem(self.level + level, self.depth) * 2 + target)

    def rank(self, first, second, level, owner=None):
        row, column = self.device(first, second, level, owner)
        return row * self.fsdp + column

    def greet(self):
        barrier = pltpu.get_barrier_semaphore()
        peers = [self.device(0, 0, 0, None, 1 - self.core)]
        peers += [self.device(k, 0, 0) for k in range(1, self.side)]
        peers += [self.device(0, k, 0) for k in range(1, self.side)]
        peers += [self.device(0, 0, k) for k in range(1, self.depth)]
        for peer in peers:
            pl.semaphore_signal(barrier, inc=1, device_id=peer, device_id_type=MESH)
        pl.semaphore_wait(barrier, len(peers))

    def number(self, first, second, level):
        return (second * self.side + first) * self.depth + level


def gather_kernel(side, fsdp, *refs):
    kinds = 2
    shards, wholes = refs[:kinds], refs[kinds : 2 * kinds]
    wired, paired, sent, kept = refs[2 * kinds :]
    here = Place(side, fsdp)
    depth = here.depth
    half = side * side * depth
    own = here.rank(0, 0, 0)
    local = [
        pltpu.make_async_copy(shards[i], wholes[i].at[own], kept.at[i]) for i in range(kinds)
    ]
    here.greet()

    def push(origin, hop):
        first, second, level = origin
        slot = here.rank(first, second, level)
        for i in range(kinds):
            source = shards[i] if origin == (0, 0, 0) else wholes[i].at[slot]
            if hop is None:
                peer = here.device(0, 0, 0, None, 1 - here.core)
                arrival = paired.at[here.number(first, second, level), i]
            else:
                peer = here.device(*hop)
                arrival = wired.at[
                    here.number(
                        (first - hop[0]) % side, (second - hop[1]) % side, (level - hop[2]) % depth
                    ),
                    i,
                ]
            pltpu.make_async_remote_copy(
                src_ref=source,
                dst_ref=wholes[i].at[slot],
                send_sem=sent.at[i],
                recv_sem=arrival,
                device_id=peer,
                device_id_type=MESH,
            ).start()

    def arrive(origin, sems, owner):
        slot = here.rank(*origin, owner)
        for i in range(kinds):
            pltpu.make_async_copy(
                wholes[i].at[slot], wholes[i].at[slot], sems.at[here.number(*origin), i]
            ).wait()

    first_hops = [(k, 0, 0) for k in range(1, side)]
    second_hops = [(0, k, 0) for k in range(1, side)]
    level_hops = [(0, 0, k) for k in range(1, depth)]
    for hop in second_hops + first_hops + level_hops + [None]:
        push((0, 0, 0), hop)
    for copy in local:
        copy.start()
    for level in range(1, depth):
        arrive((0, 0, level), wired, here.core)
        for hop in second_hops + first_hops + [None]:
            push((0, 0, level), hop)
    for level in range(depth):
        for first in range(1, side):
            arrive((first, 0, level), wired, here.core)
            for hop in second_hops + [None]:
                push((first, 0, level), hop)
    for first in range(side):
        for level in range(depth):
            for second in range(1, side):
                arrive((first, second, level), wired, here.core)
                push((first, second, level), None)
    for second in range(side):
        for first in range(side):
            for level in range(depth):
                arrive((first, second, level), paired, 1 - here.core)
    for copy in local:
        copy.wait()
    for i in range(kinds):
        every = wholes[i].at[pl.ds(0, 2 * half - 1)]
        pltpu.make_async_copy(every, every, sent.at[i]).wait()


def gather_shards(shards, side, fsdp):
    count = side * side * fsdp
    half = count // 2
    return pl.pallas_call(
        functools.partial(gather_kernel, side, fsdp),
        out_shape=[jax.ShapeDtypeStruct((count, *x.shape), x.dtype) for x in shards],
        in_specs=[pl.BlockSpec(memory_space=pltpu.VMEM)] * len(shards),
        out_specs=[pl.BlockSpec(memory_space=pl.ANY)] * len(shards),
        scratch_shapes=[
            pltpu.SemaphoreType.DMA((half, len(shards))),
            pltpu.SemaphoreType.DMA((half, len(shards))),
            pltpu.SemaphoreType.DMA((len(shards),)),
            pltpu.SemaphoreType.DMA((len(shards),)),
        ],
        compiler_params=pltpu.CompilerParams(collective_id=0, has_side_effects=True),
    )(*shards)


def scatter_kernel(side, fsdp, *refs):
    parts, (total,) = refs[:5], refs[5:6]
    mine, pair, one, two, three = refs[6:11]
    load_sem, pair_sem, wire_sem, sent_pair, sent = refs[11:]
    here = Place(side, fsdp)
    depth, rows = here.depth, total.shape[0]
    wide = total.shape[1]
    here.greet()

    pieces, at = [], 0
    for part in parts:
        for block in range(part.shape[1] // rows):
            pieces.append((part, block * rows, at, part.shape[2]))
            at += part.shape[2]

    firsts = list(range(1, side)) + [0]
    levels = list(range(1, depth)) + [0]
    order = [(f, s, k) for s in firsts for f in firsts for k in levels]
    for first, second, level in order:
        index = here.number(first, second, level)
        theirs = here.rank(first, second, level, 1 - here.core)
        ours = here.rank(first, second, level)
        for part, row, column, width in pieces:
            pltpu.make_async_remote_copy(
                src_ref=part.at[theirs, pl.ds(row, rows)],
                dst_ref=pair.at[index, :, pl.ds(column, width)],
                send_sem=sent_pair,
                recv_sem=pair_sem.at[index],
                device_id=here.device(0, 0, 0, None, 1 - here.core),
                device_id_type=MESH,
            ).start()
        for part, row, column, width in pieces:
            pltpu.make_async_copy(
                part.at[ours, pl.ds(row, rows)],
                mine.at[index, :, pl.ds(column, width)],
                load_sem.at[index],
            ).start()

    def send(index, target, slot, number, hop):
        pltpu.make_async_remote_copy(
            src_ref=mine.at[index],
            dst_ref=target.at[slot],
            send_sem=sent.at[index],
            recv_sem=wire_sem.at[number],
            device_id=here.device(*hop),
            device_id_type=MESH,
        ).start()

    def landed(block, sem):
        pltpu.make_async_copy(block, block, sem).wait()

    second_slot = lambda second, first, level: ((second - 1) * side + first) * depth + level
    first_slot = lambda first, level: (first - 1) * depth + level
    base_two = (side - 1) * side * depth
    base_three = base_two + (side - 1) * depth
    for first, second, level in order:
        index = here.number(first, second, level)
        landed(mine.at[index], load_sem.at[index])
        landed(pair.at[index], pair_sem.at[index])
        terms = [mine.at[index], pair.at[index]]
        if second == 0:
            for k in range(1, side):
                slot = second_slot(k, first, level)
                landed(one.at[slot], wire_sem.at[slot])
                terms.append(one.at[slot])
            if first == 0:
                for k in range(1, side):
                    slot = first_slot(k, level)
                    landed(two.at[slot], wire_sem.at[base_two + slot])
                    terms.append(two.at[slot])
                if level == 0:
                    for k in range(1, depth):
                        landed(three.at[k - 1], wire_sem.at[base_three + k - 1])
                        terms.append(three.at[k - 1])
        last = (first, second, level) == (0, 0, 0)

        @pl.loop(0, wide // STEP_WIDE)
        def _(step):
            columns = pl.ds(pl.multiple_of(step * STEP_WIDE, LANES), STEP_WIDE)
            value = terms[0][:, columns].astype(jnp.float32)
            for term in terms[1:]:
                value = value + term[:, columns].astype(jnp.float32)
            if last:
                total[:, columns] = value
            else:
                mine[index, :, columns] = value.astype(jnp.bfloat16)

        if second:
            slot = second_slot(second, first, level)
            send(index, one, slot, slot, (0, second, 0))
        elif first:
            slot = first_slot(first, level)
            send(index, two, slot, base_two + slot, (first, 0, 0))
        elif level:
            send(index, three, level - 1, base_three + level - 1, (0, 0, level))
    landed(pair, sent_pair)
    for first, second, level in order[:-1]:
        index = here.number(first, second, level)
        landed(mine.at[index], sent.at[index])


def scatter_sums(parts, side, fsdp):
    depth = fsdp // 2
    half, rows = side * side * depth, parts[0].shape[1]
    wide = sum(x.shape[1] * x.shape[2] for x in parts) // rows
    stages = [(side - 1) * side * depth, (side - 1) * depth, depth - 1]
    return pl.pallas_call(
        functools.partial(scatter_kernel, side, fsdp),
        out_shape=jax.ShapeDtypeStruct((rows, wide), jnp.float32),
        in_specs=[pl.BlockSpec(memory_space=pl.ANY)] * 5,
        out_specs=pl.BlockSpec(memory_space=pltpu.VMEM),
        scratch_shapes=[
            pltpu.VMEM((n, rows, wide), jnp.bfloat16) for n in [half, half, *stages]
        ]
        + [
            pltpu.SemaphoreType.DMA((half,)),
            pltpu.SemaphoreType.DMA((half,)),
            pltpu.SemaphoreType.DMA((sum(stages),)),
            pltpu.SemaphoreType.DMA,
            pltpu.SemaphoreType.DMA((half,)),
        ],
        compiler_params=pltpu.CompilerParams(
            collective_id=1, has_side_effects=True, vmem_limit_bytes=56 << 20
        ),
    )(*parts)


def gather_all(w_qkv, w_out, w_up, w_down, vectors, side, fsdp):
    rows, count = w_qkv.shape[0], side * side * fsdp
    low = [x.astype(jnp.bfloat16) for x in (w_qkv, w_out, w_up, w_down, vectors)]
    vec = jnp.pad(low[4], (0, rows * LANES - vectors.shape[0])).reshape(rows, LANES)
    packed, full_down = gather_shards(
        (jnp.concatenate([low[0], low[1], low[2], vec], axis=1), low[3]), side, fsdp
    )
    packed = packed.reshape(count * rows, -1)
    ends = [w_qkv.shape[1], w_out.shape[1], w_up.shape[1]]
    one, two, three = ends[0], ends[0] + ends[1], sum(ends)
    full_vec = packed[:, three:].reshape(count, rows * LANES)[:, : vectors.shape[0]].reshape(-1)
    return (
        packed[:, :one],
        packed[:, one:two],
        packed[:, two:three],
        full_down.reshape(-1, w_down.shape[1]),
        full_vec,
    )


def scatter_all(local_qkv, local_out, local_up, local_down, local_vec, side, fsdp):
    count = side * side * fsdp
    rows, down_rows = local_qkv.shape[0] // count, local_down.shape[0] // count
    vec_size = local_vec.shape[0] // count
    vec = jnp.pad(
        local_vec.reshape(count, vec_size), ((0, 0), (0, rows * LANES - vec_size))
    ).reshape(count, rows, LANES)
    vec = jnp.pad(vec, ((0, 0), (0, 0), (0, VEC_WIDE - LANES)))
    parts = [x.reshape(count, x.shape[0] // count, x.shape[1]) for x in (local_qkv, local_out, local_up)]
    parts += [vec, local_down.reshape(count, down_rows, -1)]
    total = scatter_sums([x.astype(jnp.bfloat16) for x in parts], side, fsdp)
    outs, at = [], 0
    for part in parts:
        width = part.shape[1] * part.shape[2] // rows
        outs.append(total[:, at : at + width])
        at += width
    down = outs[4].reshape(rows, down_rows // rows, -1).swapaxes(0, 1).reshape(down_rows, -1)
    return outs[0], outs[1], outs[2], down, outs[3][:, :LANES].reshape(-1)[:vec_size]


def per_device(
    tokens,
    cotangent,
    segments,
    w_qkv,
    w_out,
    w_up,
    w_down,
    vectors,
    first_qkv,
    first_out,
    first_up,
    first_down,
    first_vec,
    second_qkv,
    second_out,
    second_up,
    second_down,
    second_vec,
):
    device_count = lax.axis_size(("dp", "fsdp"))
    segment = segments[0]
    allowed = doc_mask(segment)
    cosine_part, sine_part = rotary_tables(segment)
    axes = ("dp", "fsdp")
    fsdp = lax.axis_size("fsdp")
    side = math.isqrt(lax.axis_size("dp"))
    direct = (
        side * side == lax.axis_size("dp")
        and fsdp % 2 == 0
        and w_qkv.shape[0] % 8 == 0
        and w_down.shape[0] % w_qkv.shape[0] == 0
        and vectors.shape[0] <= w_qkv.shape[0] * LANES
    )
    if direct:
        full_qkv, full_out, full_up, full_down, full_vec = gather_all(
            w_qkv, w_out, w_up, w_down, vectors, side, fsdp
        )
    else:
        full_qkv, full_out, full_up, full_down, full_vec = (
            lax.all_gather(x.astype(jnp.bfloat16), axes, axis=0, tiled=True)
            for x in (w_qkv, w_out, w_up, w_down, vectors)
        )
    output, saved = forward_pass(
        tokens, allowed, cosine_part, sine_part, full_qkv, full_out, full_up, full_down, full_vec
    )
    grad_tokens, local_qkv, local_out, local_up, local_down, local_vec = backward_pass(
        saved,
        cotangent,
        allowed,
        cosine_part,
        sine_part,
        full_qkv,
        full_out,
        full_up,
        full_down,
        full_vec,
    )
    factor = 1.0 / math.sqrt(device_count * tokens.shape[0])
    local = (local_qkv, local_out, local_up, local_down, local_vec)
    if direct:
        summed_qkv, summed_out, summed_up, summed_down, summed_vec = scatter_all(*local, side, fsdp)
    else:
        summed_qkv, summed_out, summed_up, summed_down, summed_vec = (
            lax.psum_scatter(x, axes, scatter_dimension=0, tiled=True) for x in local
        )
    grad_w_qkv = summed_qkv * factor
    grad_w_out = summed_out * factor
    grad_vectors = summed_vec * factor
    grad_w_up = summed_up * factor
    grad_w_down = summed_down * factor
    new_w_qkv, new_first_qkv, new_second_qkv = adam_update(
        w_qkv, grad_w_qkv, first_qkv, second_qkv, rate_matrix, decay_matrix
    )
    new_w_out, new_first_out, new_second_out = adam_update(
        w_out, grad_w_out, first_out, second_out, rate_matrix, decay_matrix
    )
    new_w_up, new_first_up, new_second_up = adam_update(
        w_up, grad_w_up, first_up, second_up, rate_matrix, decay_matrix
    )
    new_w_down, new_first_down, new_second_down = adam_update(
        w_down, grad_w_down, first_down, second_down, rate_matrix, decay_matrix
    )
    new_vectors, new_first_vec, new_second_vec = adam_update(
        vectors, grad_vectors, first_vec, second_vec, rate_vector, 0.0
    )
    return (
        output,
        grad_tokens,
        grad_w_qkv,
        grad_w_out,
        grad_w_up,
        grad_w_down,
        grad_vectors,
        new_w_qkv,
        new_w_out,
        new_w_up,
        new_w_down,
        new_vectors,
        new_first_qkv,
        new_first_out,
        new_first_up,
        new_first_down,
        new_first_vec,
        new_second_qkv,
        new_second_out,
        new_second_up,
        new_second_down,
        new_second_vec,
    )


def solution(mesh):
    placed = (
        P(("dp", "fsdp"), None),
        P(("dp", "fsdp"), None),
        P(("dp", "fsdp"), None),
        P(("dp", "fsdp"), None),
        P(("dp", "fsdp"), None),
        P(("dp", "fsdp"), None),
        P(("dp", "fsdp"), None),
        P(("dp", "fsdp")),
        P(("dp", "fsdp"), None),
        P(("dp", "fsdp"), None),
        P(("dp", "fsdp"), None),
        P(("dp", "fsdp"), None),
        P(("dp", "fsdp")),
        P(("dp", "fsdp"), None),
        P(("dp", "fsdp"), None),
        P(("dp", "fsdp"), None),
        P(("dp", "fsdp"), None),
        P(("dp", "fsdp")),
    )
    return jax.shard_map(
        per_device,
        mesh=mesh,
        in_specs=placed,
        out_specs=(
            P(("dp", "fsdp"), None),
            P(("dp", "fsdp"), None),
            P(("dp", "fsdp"), None),
            P(("dp", "fsdp"), None),
            P(("dp", "fsdp"), None),
            P(("dp", "fsdp"), None),
            P(("dp", "fsdp")),
            P(("dp", "fsdp"), None),
            P(("dp", "fsdp"), None),
            P(("dp", "fsdp"), None),
            P(("dp", "fsdp"), None),
            P(("dp", "fsdp")),
            P(("dp", "fsdp"), None),
            P(("dp", "fsdp"), None),
            P(("dp", "fsdp"), None),
            P(("dp", "fsdp"), None),
            P(("dp", "fsdp")),
            P(("dp", "fsdp"), None),
            P(("dp", "fsdp"), None),
            P(("dp", "fsdp"), None),
            P(("dp", "fsdp"), None),
            P(("dp", "fsdp")),
        ),
        check_vma=False,
    )
```

```python
import functools
import math

import jax
import jax.numpy as jnp
from jax import lax
from jax.experimental import pallas as pl
from jax.experimental.pallas import tpu as pltpu
from jax.sharding import PartitionSpec as P

D = 768
HEADS = 12
HEAD_DIM = 64
ROT = 16
STEP = 3


eps_norm = 1e-05
beta_first = 0.9
beta_second = 0.95
adam_epsilon = 1e-08
rate_matrix = 0.008
rate_vector = 0.1
decay_matrix = 0.01
rotary_base = 10000.0
mask_fill = -1e30


def layer_norm(inputs, gain_row, offset):
    center = inputs - jnp.mean(inputs, axis=-1, keepdims=True)
    inv_sigma = lax.rsqrt(jnp.mean(center * center, axis=-1, keepdims=True) + eps_norm)
    normed = center * inv_sigma
    return (normed, inv_sigma, normed * gain_row + offset)


def layer_norm_back(grad_norm, normed, inv_sigma, gain_row):
    scaled = grad_norm * gain_row
    return inv_sigma * (
        scaled
        - jnp.mean(scaled, axis=-1, keepdims=True)
        - normed * jnp.mean(scaled * normed, axis=-1, keepdims=True)
    )


def gelu_value(inputs):
    return 0.5 * inputs * (1.0 + jax.scipy.special.erf(inputs * (1.0 / math.sqrt(2.0))))


def gelu_slope(inputs):
    cumulative = 0.5 * (1.0 + jax.scipy.special.erf(inputs * (1.0 / math.sqrt(2.0))))
    return cumulative + inputs * jnp.exp(-0.5 * inputs * inputs) * (1.0 / math.sqrt(2.0 * math.pi))


def rotary_tables(segment):
    rows_here = segment.shape[0]
    earlier = jnp.sum((segment[None, :] < segment[:, None]).astype(jnp.int32), axis=1)
    position = jnp.arange(rows_here, dtype=jnp.int32) - earlier
    half_rot = ROT // 2
    inverse = rotary_base ** (-2.0 * jnp.arange(half_rot, dtype=jnp.float32) / ROT)
    angles = position.astype(jnp.float32)[:, None] * inverse[None, :]
    return (jnp.cos(angles)[:, None, :], jnp.sin(angles)[:, None, :])


def rotate(tensor, cosine_part, sine_part):
    half_rot = ROT // 2
    front_part = tensor[..., :half_rot]
    middle = tensor[..., half_rot:ROT]
    remain = tensor[..., ROT:]
    return jnp.concatenate(
        [
            front_part * cosine_part - middle * sine_part,
            middle * cosine_part + front_part * sine_part,
            remain,
        ],
        axis=-1,
    )


def rotate_back(tensor, cosine_part, sine_part):
    half_rot = ROT // 2
    front_part = tensor[..., :half_rot]
    middle = tensor[..., half_rot:ROT]
    remain = tensor[..., ROT:]
    return jnp.concatenate(
        [
            front_part * cosine_part + middle * sine_part,
            middle * cosine_part - front_part * sine_part,
            remain,
        ],
        axis=-1,
    )


def doc_mask(segment):
    row_index = jnp.arange(segment.shape[0], dtype=jnp.int32)
    return (segment[:, None] == segment[None, :]) & (row_index[None, :] <= row_index[:, None])


def masked_scores(queries, key_rot, allowed):
    scores = jnp.einsum("qhd,khd->hqk", queries, key_rot, preferred_element_type=jnp.float32) * (
        1.0 / math.sqrt(HEAD_DIM)
    )
    return jnp.where(allowed[None, :, :], scores, mask_fill)


def forward_pass(
    tokens, allowed, cosine_part, sine_part, full_qkv, full_out, full_up, full_down, full_vec
):
    rows_here = tokens.shape[0]
    vec_table = full_vec.astype(jnp.float32).reshape(13, D)
    inputs = tokens.astype(jnp.float32)
    normed_one, sigma_one, hidden_one = layer_norm(inputs, vec_table[0], vec_table[1])
    normed_two, sigma_two, hidden_two = layer_norm(inputs, vec_table[2], vec_table[3])
    hidden_one = hidden_one.astype(jnp.bfloat16)
    hidden_two = hidden_two.astype(jnp.bfloat16)
    projected = jnp.dot(hidden_one, full_qkv, preferred_element_type=jnp.float32) + vec_table[
        4:7
    ].reshape(-1)
    queries = rotate(
        projected[:, :D].reshape(rows_here, HEADS, HEAD_DIM), cosine_part, sine_part
    ).astype(jnp.bfloat16)
    key_rot = rotate(
        projected[:, D : 2 * D].reshape(rows_here, HEADS, HEAD_DIM), cosine_part, sine_part
    ).astype(jnp.bfloat16)
    values = projected[:, 2 * D :].reshape(rows_here, HEADS, HEAD_DIM).astype(jnp.bfloat16)
    scores = masked_scores(queries, key_rot, allowed)
    top_score = jnp.max(scores, axis=-1, keepdims=True)
    log_total = top_score + jnp.log(jnp.sum(jnp.exp(scores - top_score), axis=-1, keepdims=True))
    soft_weights = jnp.exp(scores - log_total).astype(jnp.bfloat16)
    context = (
        jnp.einsum("hqk,khd->qhd", soft_weights, values, preferred_element_type=jnp.float32)
        .reshape(rows_here, D)
        .astype(jnp.bfloat16)
    )
    attended = jnp.dot(context, full_out, preferred_element_type=jnp.float32) + vec_table[7]
    up_proj = jnp.dot(hidden_two, full_up, preferred_element_type=jnp.float32) + vec_table[
        8:12
    ].reshape(-1)
    activated = gelu_value(up_proj).astype(jnp.bfloat16)
    feed_out = jnp.dot(activated, full_down, preferred_element_type=jnp.float32) + vec_table[12]
    output = (inputs + attended + feed_out).astype(jnp.bfloat16)
    saved = (
        normed_one,
        sigma_one,
        hidden_one,
        normed_two,
        sigma_two,
        hidden_two,
        queries,
        key_rot,
        values,
        log_total,
        context,
        up_proj,
        activated,
    )
    return (output, saved)


def backward_pass(
    saved,
    cotangent,
    allowed,
    cosine_part,
    sine_part,
    back_qkv,
    back_out,
    back_up,
    back_down,
    back_vec,
):
    (
        normed_one,
        sigma_one,
        hidden_one,
        normed_two,
        sigma_two,
        hidden_two,
        queries,
        key_rot,
        values,
        log_total,
        context,
        up_proj,
        activated,
    ) = saved
    rows_here = cotangent.shape[0]
    vec_table = back_vec.astype(jnp.float32).reshape(13, D)
    grad_out = cotangent.astype(jnp.float32)
    grad_w_down = jnp.dot(activated.T, cotangent, preferred_element_type=jnp.float32)
    grad_act = jnp.dot(cotangent, back_down.T, preferred_element_type=jnp.float32)
    grad_up = grad_act * gelu_slope(up_proj)
    grad_up_low = grad_up.astype(jnp.bfloat16)
    grad_w_up = jnp.dot(hidden_two.T, grad_up_low, preferred_element_type=jnp.float32)
    grad_hidden_two = jnp.dot(grad_up_low, back_up.T, preferred_element_type=jnp.float32)
    grad_w_out = jnp.dot(context.T, cotangent, preferred_element_type=jnp.float32)
    grad_context = (
        jnp.dot(cotangent, back_out.T, preferred_element_type=jnp.float32)
        .astype(jnp.bfloat16)
        .reshape(rows_here, HEADS, HEAD_DIM)
    )
    again_scores = masked_scores(queries, key_rot, allowed)
    probs_full = jnp.exp(again_scores - log_total)
    probs_low = probs_full.astype(jnp.bfloat16)
    grad_probs = jnp.einsum(
        "qhd,khd->hqk", grad_context, values, preferred_element_type=jnp.float32
    )
    row_inner = jnp.sum(probs_full * grad_probs, axis=-1, keepdims=True)
    grad_scores = (probs_full * (grad_probs - row_inner) * (1.0 / math.sqrt(HEAD_DIM))).astype(
        jnp.bfloat16
    )
    grad_queries = jnp.einsum(
        "hqk,khd->qhd", grad_scores, key_rot, preferred_element_type=jnp.float32
    )
    grad_keys = jnp.einsum("hqk,qhd->khd", grad_scores, queries, preferred_element_type=jnp.float32)
    grad_values = jnp.einsum(
        "hqk,qhd->khd", probs_low, grad_context, preferred_element_type=jnp.float32
    )
    grad_projected = jnp.concatenate(
        [
            rotate_back(grad_queries, cosine_part, sine_part).reshape(rows_here, D),
            rotate_back(grad_keys, cosine_part, sine_part).reshape(rows_here, D),
            grad_values.reshape(rows_here, D),
        ],
        axis=1,
    )
    grad_proj_low = grad_projected.astype(jnp.bfloat16)
    grad_w_qkv = jnp.dot(hidden_one.T, grad_proj_low, preferred_element_type=jnp.float32)
    grad_hidden_one = jnp.dot(grad_proj_low, back_qkv.T, preferred_element_type=jnp.float32)
    grad_table = jnp.concatenate(
        [
            jnp.sum(grad_hidden_one * normed_one, axis=0)[None],
            jnp.sum(grad_hidden_one, axis=0)[None],
            jnp.sum(grad_hidden_two * normed_two, axis=0)[None],
            jnp.sum(grad_hidden_two, axis=0)[None],
            jnp.sum(grad_projected, axis=0).reshape(3, D),
            jnp.sum(grad_out, axis=0)[None],
            jnp.sum(grad_up, axis=0).reshape(4, D),
            jnp.sum(grad_out, axis=0)[None],
        ],
        axis=0,
    )
    grad_tokens = (
        grad_out
        + layer_norm_back(grad_hidden_one, normed_one, sigma_one, vec_table[0])
        + layer_norm_back(grad_hidden_two, normed_two, sigma_two, vec_table[2])
    ).astype(jnp.bfloat16)
    grad_table = lax.optimization_barrier(grad_table)
    return (grad_tokens, grad_w_qkv, grad_w_out, grad_w_up, grad_w_down, grad_table.reshape(-1))


def adam_update(weight, gradient, moment_one, moment_two, rate_value, decay_value):
    new_one = beta_first * moment_one + (1.0 - beta_first) * gradient
    new_two = beta_second * moment_two + (1.0 - beta_second) * gradient * gradient
    corrected_one = new_one / (1.0 - beta_first**STEP)
    corrected_two = new_two / (1.0 - beta_second**STEP)
    new_weight = weight - rate_value * (
        corrected_one / (jnp.sqrt(corrected_two) + adam_epsilon) + decay_value * weight
    )
    return (new_weight, new_one, new_two)


MESH = pl.DeviceIdType.MESH
LANES = 128
VEC_WIDE = 3 * LANES
STEP_WIDE = 5 * LANES
CHUNKS = 5


class Place:
    def __init__(self, side, fsdp):
        self.side, self.fsdp, self.depth = side, fsdp, fsdp // 2
        index, column = lax.axis_index("dp"), lax.axis_index("fsdp")
        self.core, self.level = lax.rem(column, 2), lax.div(column, 2)
        self.high, self.low = lax.div(index, side), lax.rem(index, side)

    def device(self, first, second, level, owner=None, target=None):
        owner = self.core if owner is None else owner
        target = owner if target is None else target
        one = lax.rem(self.low * (1 - owner) + self.high * owner + first, self.side)
        two = lax.rem(self.high * (1 - owner) + self.low * owner + second, self.side)
        high = two * (1 - owner) + one * owner
        low = one * (1 - owner) + two * owner
        return (high * self.side + low, lax.rem(self.level + level, self.depth) * 2 + target)

    def rank(self, first, second, level, owner=None):
        row, column = self.device(first, second, level, owner)
        return row * self.fsdp + column

    def greet(self):
        barrier = pltpu.get_barrier_semaphore()
        peers = [self.device(0, 0, 0, None, 1 - self.core)]
        peers += [self.device(k, 0, 0) for k in range(1, self.side)]
        peers += [self.device(0, k, 0) for k in range(1, self.side)]
        peers += [self.device(0, 0, k) for k in range(1, self.depth)]
        for peer in peers:
            pl.semaphore_signal(barrier, inc=1, device_id=peer, device_id_type=MESH)
        pl.semaphore_wait(barrier, len(peers))

    def number(self, first, second, level):
        return (second * self.side + first) * self.depth + level


def gather_kernel(side, fsdp, *refs):
    kinds = 3
    shards, wholes = refs[:kinds], refs[kinds : 2 * kinds]
    wired, paired, sent, kept = refs[2 * kinds :]
    here = Place(side, fsdp)
    depth = here.depth
    half = side * side * depth
    own = here.rank(0, 0, 0)
    local = [
        pltpu.make_async_copy(shards[i], wholes[i].at[own], kept.at[i]) for i in range(kinds)
    ]
    here.greet()

    def push(origin, hop, i):
        first, second, level = origin
        slot = here.rank(first, second, level)
        source = shards[i] if origin == (0, 0, 0) else wholes[i].at[slot]
        if hop is None:
            peer = here.device(0, 0, 0, None, 1 - here.core)
            arrival = paired.at[here.number(first, second, level), i]
        else:
            peer = here.device(*hop)
            arrival = wired.at[
                here.number(
                    (first - hop[0]) % side, (second - hop[1]) % side, (level - hop[2]) % depth
                ),
                i,
            ]
        pltpu.make_async_remote_copy(
            src_ref=source,
            dst_ref=wholes[i].at[slot],
            send_sem=sent.at[i],
            recv_sem=arrival,
            device_id=peer,
            device_id_type=MESH,
        ).start()

    def arrive(origin, sems, owner, i):
        slot = here.rank(*origin, owner)
        pltpu.make_async_copy(
            wholes[i].at[slot], wholes[i].at[slot], sems.at[here.number(*origin), i]
        ).wait()

    def relay(origin, hops):
        for i in range(kinds):
            arrive(origin, wired, here.core, i)
            for hop in hops:
                push(origin, hop, i)

    first_hops = [(k, 0, 0) for k in range(1, side)]
    second_hops = [(0, k, 0) for k in range(1, side)]
    level_hops = [(0, 0, k) for k in range(1, depth)]
    for i in range(kinds):
        for hop in level_hops + second_hops + first_hops + [None]:
            push((0, 0, 0), hop, i)
    for copy in local:
        copy.start()
    for level in range(1, depth + 1):
        if level < depth:
            relay((0, 0, level), second_hops + first_hops + [None])
        for first in range(1, side):
            relay((first, 0, level - 1), second_hops + [None])
    for level in range(depth):
        for first in range(side):
            for second in range(1, side):
                relay((first, second, level), [None])
    for level in range(depth):
        for second in range(side):
            for first in range(side):
                for i in range(kinds):
                    arrive((first, second, level), paired, 1 - here.core, i)
    for copy in local:
        copy.wait()
    for i in range(kinds):
        every = wholes[i].at[pl.ds(0, 2 * half - 1)]
        pltpu.make_async_copy(every, every, sent.at[i]).wait()


def gather_shards(shards, side, fsdp):
    count = side * side * fsdp
    half = count // 2
    return pl.pallas_call(
        functools.partial(gather_kernel, side, fsdp),
        out_shape=[jax.ShapeDtypeStruct((count, *x.shape), x.dtype) for x in shards],
        in_specs=[pl.BlockSpec(memory_space=pltpu.VMEM)] * len(shards),
        out_specs=[pl.BlockSpec(memory_space=pl.ANY)] * len(shards),
        scratch_shapes=[
            pltpu.SemaphoreType.DMA((half, len(shards))),
            pltpu.SemaphoreType.DMA((half, len(shards))),
            pltpu.SemaphoreType.DMA((len(shards),)),
            pltpu.SemaphoreType.DMA((len(shards),)),
        ],
        compiler_params=pltpu.CompilerParams(collective_id=0, has_side_effects=True),
    )(*shards)


def scatter_kernel(side, fsdp, *refs):
    parts, (total,) = refs[:5], refs[5:6]
    mine, pair, one, two, three = refs[6:11]
    load_sem, pair_sem, wire_sem, sent_pair, sent = refs[11:]
    here = Place(side, fsdp)
    depth, rows = here.depth, total.shape[0]
    wide = total.shape[1]
    here.greet()

    span = wide // CHUNKS
    pieces, at = [[] for _ in range(CHUNKS)], 0
    for part in parts:
        for block in range(part.shape[1] // rows):
            start, end = at, at + part.shape[2]
            while at < end:
                chunk, width = at // span, min(end, (at // span + 1) * span) - at
                pieces[chunk].append((part, block * rows, at - start, at - chunk * span, width))
                at += width

    firsts = list(range(1, side)) + [0]
    levels = list(range(1, depth)) + [0]
    order = [(f, s, k) for s in firsts for f in firsts for k in levels]
    for chunk in range(CHUNKS):
        for first, second, level in order:
            index = here.number(first, second, level)
            theirs = here.rank(first, second, level, 1 - here.core)
            ours = here.rank(first, second, level)
            for part, row, source, column, width in pieces[chunk]:
                pltpu.make_async_remote_copy(
                    src_ref=part.at[theirs, pl.ds(row, rows), pl.ds(source, width)],
                    dst_ref=pair.at[chunk, index, :, pl.ds(column, width)],
                    send_sem=sent_pair,
                    recv_sem=pair_sem.at[chunk, index],
                    device_id=here.device(0, 0, 0, None, 1 - here.core),
                    device_id_type=MESH,
                ).start()
            for part, row, source, column, width in pieces[chunk]:
                pltpu.make_async_copy(
                    part.at[ours, pl.ds(row, rows), pl.ds(source, width)],
                    mine.at[chunk, index, :, pl.ds(column, width)],
                    load_sem.at[chunk, index],
                ).start()

    def send(chunk, index, target, slot, number, hop):
        pltpu.make_async_remote_copy(
            src_ref=mine.at[chunk, index],
            dst_ref=target.at[chunk, slot],
            send_sem=sent.at[chunk, index],
            recv_sem=wire_sem.at[chunk, number],
            device_id=here.device(*hop),
            device_id_type=MESH,
        ).start()

    def landed(block, sem):
        pltpu.make_async_copy(block, block, sem).wait()

    second_slot = lambda second, first, level: ((second - 1) * side + first) * depth + level
    first_slot = lambda first, level: (first - 1) * depth + level
    base_two = (side - 1) * side * depth
    base_three = base_two + (side - 1) * depth

    def handle(chunk, first, second, level):
        index = here.number(first, second, level)
        landed(mine.at[chunk, index], load_sem.at[chunk, index])
        landed(pair.at[chunk, index], pair_sem.at[chunk, index])
        terms = [mine.at[chunk, index], pair.at[chunk, index]]
        if second == 0:
            for k in range(1, side):
                slot = second_slot(k, first, level)
                landed(one.at[chunk, slot], wire_sem.at[chunk, slot])
                terms.append(one.at[chunk, slot])
            if first == 0:
                for k in range(1, side):
                    slot = first_slot(k, level)
                    landed(two.at[chunk, slot], wire_sem.at[chunk, base_two + slot])
                    terms.append(two.at[chunk, slot])
                if level == 0:
                    for k in range(1, depth):
                        landed(three.at[chunk, k - 1], wire_sem.at[chunk, base_three + k - 1])
                        terms.append(three.at[chunk, k - 1])
        last = (first, second, level) == (0, 0, 0)

        @pl.loop(0, span // STEP_WIDE)
        def _(step):
            columns = pl.ds(pl.multiple_of(step * STEP_WIDE, LANES), STEP_WIDE)
            value = terms[0][:, columns].astype(jnp.float32)
            for term in terms[1:]:
                value = value + term[:, columns].astype(jnp.float32)
            if last:
                place = pl.ds(pl.multiple_of(chunk * span + step * STEP_WIDE, LANES), STEP_WIDE)
                total[:, place] = value
            else:
                mine[chunk, index, :, columns] = value.astype(jnp.bfloat16)

        if second:
            slot = second_slot(second, first, level)
            send(chunk, index, one, slot, slot, (0, second, 0))
        elif first:
            slot = first_slot(first, level)
            send(chunk, index, two, slot, base_two + slot, (first, 0, 0))
        elif level:
            send(chunk, index, three, level - 1, base_three + level - 1, (0, 0, level))

    stages = [[], [], [], []]
    for first, second, level in order:
        stage = 0 if second else 1 if first else 2 if level else 3
        stages[stage].append((first, second, level))
    for tick in range(CHUNKS + len(stages) + 2):
        for stage in range(len(stages)):
            chunk = tick - stage
            if 0 <= chunk < CHUNKS:
                for item in stages[stage]:
                    handle(chunk, *item)
    landed(pair, sent_pair)
    for chunk in range(CHUNKS):
        for first, second, level in order[:-1]:
            index = here.number(first, second, level)
            landed(mine.at[chunk, index], sent.at[chunk, index])


def scatter_sums(parts, side, fsdp):
    depth = fsdp // 2
    half, rows = side * side * depth, parts[0].shape[1]
    wide = sum(x.shape[1] * x.shape[2] for x in parts) // rows
    stages = [(side - 1) * side * depth, (side - 1) * depth, depth - 1]
    return pl.pallas_call(
        functools.partial(scatter_kernel, side, fsdp),
        out_shape=jax.ShapeDtypeStruct((rows, wide), jnp.float32),
        in_specs=[pl.BlockSpec(memory_space=pl.ANY)] * 5,
        out_specs=pl.BlockSpec(memory_space=pltpu.VMEM),
        scratch_shapes=[
            pltpu.VMEM((CHUNKS, n, rows, wide // CHUNKS), jnp.bfloat16)
            for n in [half, half, *stages]
        ]
        + [
            pltpu.SemaphoreType.DMA((CHUNKS, half)),
            pltpu.SemaphoreType.DMA((CHUNKS, half)),
            pltpu.SemaphoreType.DMA((CHUNKS, sum(stages))),
            pltpu.SemaphoreType.DMA,
            pltpu.SemaphoreType.DMA((CHUNKS, half)),
        ],
        compiler_params=pltpu.CompilerParams(
            collective_id=1, has_side_effects=True, vmem_limit_bytes=56 << 20
        ),
    )(*parts)


def gather_all(w_qkv, w_out, w_up, w_down, vectors, side, fsdp):
    rows, count = w_qkv.shape[0], side * side * fsdp
    low = [x.astype(jnp.bfloat16) for x in (w_qkv, w_out, w_up, w_down, vectors)]
    vec = jnp.pad(low[4], (0, rows * LANES - vectors.shape[0])).reshape(rows, LANES)
    packed, full_up, full_down = gather_shards(
        (jnp.concatenate([low[0], low[1], vec], axis=1), low[2], low[3]), side, fsdp
    )
    packed = packed.reshape(count * rows, -1)
    one, two = w_qkv.shape[1], w_qkv.shape[1] + w_out.shape[1]
    full_vec = packed[:, two:].reshape(count, rows * LANES)[:, : vectors.shape[0]].reshape(-1)
    return (
        packed[:, :one],
        packed[:, one:two],
        full_up.reshape(-1, w_up.shape[1]),
        full_down.reshape(-1, w_down.shape[1]),
        full_vec,
    )


def scatter_all(local_qkv, local_out, local_up, local_down, local_vec, side, fsdp):
    count = side * side * fsdp
    rows, down_rows = local_qkv.shape[0] // count, local_down.shape[0] // count
    vec_size = local_vec.shape[0] // count
    vec = jnp.pad(
        local_vec.reshape(count, vec_size), ((0, 0), (0, rows * LANES - vec_size))
    ).reshape(count, rows, LANES)
    vec = jnp.pad(vec, ((0, 0), (0, 0), (0, VEC_WIDE - LANES)))
    parts = [x.reshape(count, x.shape[0] // count, x.shape[1]) for x in (local_qkv, local_out, local_up)]
    parts += [vec, local_down.reshape(count, down_rows, -1)]
    total = scatter_sums([x.astype(jnp.bfloat16) for x in parts], side, fsdp)
    outs, at = [], 0
    for part in parts:
        width = part.shape[1] * part.shape[2] // rows
        outs.append(total[:, at : at + width])
        at += width
    down = outs[4].reshape(rows, down_rows // rows, -1).swapaxes(0, 1).reshape(down_rows, -1)
    return outs[0], outs[1], outs[2], down, outs[3][:, :LANES].reshape(-1)[:vec_size]


def per_device(
    tokens,
    cotangent,
    segments,
    w_qkv,
    w_out,
    w_up,
    w_down,
    vectors,
    first_qkv,
    first_out,
    first_up,
    first_down,
    first_vec,
    second_qkv,
    second_out,
    second_up,
    second_down,
    second_vec,
):
    device_count = lax.axis_size(("dp", "fsdp"))
    segment = segments[0]
    allowed = doc_mask(segment)
    cosine_part, sine_part = rotary_tables(segment)
    axes = ("dp", "fsdp")
    fsdp = lax.axis_size("fsdp")
    side = math.isqrt(lax.axis_size("dp"))
    direct = (
        side * side == lax.axis_size("dp")
        and fsdp % 2 == 0
        and w_qkv.shape[0] % 8 == 0
        and w_down.shape[0] % w_qkv.shape[0] == 0
        and vectors.shape[0] <= w_qkv.shape[0] * LANES
    )
    if direct:
        full_qkv, full_out, full_up, full_down, full_vec = gather_all(
            w_qkv, w_out, w_up, w_down, vectors, side, fsdp
        )
    else:
        full_qkv, full_out, full_up, full_down, full_vec = (
            lax.all_gather(x.astype(jnp.bfloat16), axes, axis=0, tiled=True)
            for x in (w_qkv, w_out, w_up, w_down, vectors)
        )
    output, saved = forward_pass(
        tokens, allowed, cosine_part, sine_part, full_qkv, full_out, full_up, full_down, full_vec
    )
    grad_tokens, local_qkv, local_out, local_up, local_down, local_vec = backward_pass(
        saved,
        cotangent,
        allowed,
        cosine_part,
        sine_part,
        full_qkv,
        full_out,
        full_up,
        full_down,
        full_vec,
    )
    factor = 1.0 / math.sqrt(device_count * tokens.shape[0])
    local = (local_qkv, local_out, local_up, local_down, local_vec)
    if direct:
        summed_qkv, summed_out, summed_up, summed_down, summed_vec = scatter_all(*local, side, fsdp)
    else:
        summed_qkv, summed_out, summed_up, summed_down, summed_vec = (
            lax.psum_scatter(x, axes, scatter_dimension=0, tiled=True) for x in local
        )
    grad_w_qkv = summed_qkv * factor
    grad_w_out = summed_out * factor
    grad_vectors = summed_vec * factor
    grad_w_up = summed_up * factor
    grad_w_down = summed_down * factor
    new_w_qkv, new_first_qkv, new_second_qkv = adam_update(
        w_qkv, grad_w_qkv, first_qkv, second_qkv, rate_matrix, decay_matrix
    )
    new_w_out, new_first_out, new_second_out = adam_update(
        w_out, grad_w_out, first_out, second_out, rate_matrix, decay_matrix
    )
    new_w_up, new_first_up, new_second_up = adam_update(
        w_up, grad_w_up, first_up, second_up, rate_matrix, decay_matrix
    )
    new_w_down, new_first_down, new_second_down = adam_update(
        w_down, grad_w_down, first_down, second_down, rate_matrix, decay_matrix
    )
    new_vectors, new_first_vec, new_second_vec = adam_update(
        vectors, grad_vectors, first_vec, second_vec, rate_vector, 0.0
    )
    return (
        output,
        grad_tokens,
        grad_w_qkv,
        grad_w_out,
        grad_w_up,
        grad_w_down,
        grad_vectors,
        new_w_qkv,
        new_w_out,
        new_w_up,
        new_w_down,
        new_vectors,
        new_first_qkv,
        new_first_out,
        new_first_up,
        new_first_down,
        new_first_vec,
        new_second_qkv,
        new_second_out,
        new_second_up,
        new_second_down,
        new_second_vec,
    )


def solution(mesh):
    placed = (
        P(("dp", "fsdp"), None),
        P(("dp", "fsdp"), None),
        P(("dp", "fsdp"), None),
        P(("dp", "fsdp"), None),
        P(("dp", "fsdp"), None),
        P(("dp", "fsdp"), None),
        P(("dp", "fsdp"), None),
        P(("dp", "fsdp")),
        P(("dp", "fsdp"), None),
        P(("dp", "fsdp"), None),
        P(("dp", "fsdp"), None),
        P(("dp", "fsdp"), None),
        P(("dp", "fsdp")),
        P(("dp", "fsdp"), None),
        P(("dp", "fsdp"), None),
        P(("dp", "fsdp"), None),
        P(("dp", "fsdp"), None),
        P(("dp", "fsdp")),
    )
    return jax.shard_map(
        per_device,
        mesh=mesh,
        in_specs=placed,
        out_specs=(
            P(("dp", "fsdp"), None),
            P(("dp", "fsdp"), None),
            P(("dp", "fsdp"), None),
            P(("dp", "fsdp"), None),
            P(("dp", "fsdp"), None),
            P(("dp", "fsdp"), None),
            P(("dp", "fsdp")),
            P(("dp", "fsdp"), None),
            P(("dp", "fsdp"), None),
            P(("dp", "fsdp"), None),
            P(("dp", "fsdp"), None),
            P(("dp", "fsdp")),
            P(("dp", "fsdp"), None),
            P(("dp", "fsdp"), None),
            P(("dp", "fsdp"), None),
            P(("dp", "fsdp"), None),
            P(("dp", "fsdp")),
            P(("dp", "fsdp"), None),
            P(("dp", "fsdp"), None),
            P(("dp", "fsdp"), None),
            P(("dp", "fsdp"), None),
            P(("dp", "fsdp")),
        ),
        check_vma=False,
    )
```
